256 devices in a mesh: gx: 16 (over x, z_hi), gy: 4 (over y), gz: 4 (over z_lo, core).
Axes of the slice: x: 4, y: 4, z: 8 (z_hi: 4, z_lo: 2; z = z_hi * 2 + z_lo), core: 2. Of those that a mesh axis runs over, the one named last changes fastest.
Arguments:
- flow_field: bfloat16 [512, 256, 2048], P('gx', 'gy', 'gz'), may hold values from -96 to 96
- left_x: bfloat16 [512, 128], P('gx'), may hold values from -0.0234375 to 0.0234375
- last_x: bfloat16 [512, 128], P('gx'), may hold values from -0.25 to 0.25
- last_y: bfloat16 [256, 128], P('gy'), may hold values from -0.005859375 to 0.005859375
- right_y: bfloat16 [256, 256], P('gy'), may hold values from -0.375 to 0.375
- right_m: bfloat16 [2048, 256], P('gz'), may hold values from -0.125 to 0.125
- last_m: bfloat16 [2048, 256], P('gz'), may hold values from -0.125 to 0.125
Outputs:
- core_first: float32 [512, 128], P('gx')
- core_middle: float32 [128, 256, 128], P(('gx', 'gz'), 'gy')
- core_last: float32 [128, 2048], P(None, 'gz')
The draws below stay inside these ranges and needn't reach their ends.
All inputs are finite; a program needn't handle non-finite values.
Results may differ from the reference program's by a relative error of at most 0.0053.
Values sent between devices are 32-bit elements; how exact they have to be, the bound alone decides.
A program may use at most 64 MiB of HBM per device.

```python
import jax
import jax.numpy as jnp
from jax import lax

R = 128
L = 256
NX = 512
NY = 256
M = 2048


def shard_levels(own_key, shape, cuts, smallest, high):
    factor_of = 1.0
    for axis_at, parts in cuts:
        draws = jax.random.uniform(jax.random.fold_in(jax.random.fold_in(own_key, 6), axis_at), (parts,), jnp.float32, smallest / len(cuts), high / len(cuts))
        factor_of = factor_of * jnp.repeat(jnp.exp(draws), shape[axis_at] // parts).reshape((-1,) + (1,) * (len(shape) - 1 - axis_at))
    return factor_of


def centred(key, extent, width, bound, cuts=(), held_as=jnp.bfloat16):
    factor_of = shard_levels(key, extent, cuts, -0.22, 0.18) if cuts else 1.0
    array = jax.random.normal(key, extent, jnp.float32) * width * factor_of
    return jnp.minimum(jnp.maximum(array, -bound), bound).astype(held_as)


def setup_inputs(seed: int = 0) -> dict:
    arg_keys = jax.random.split(jax.random.key(seed), 8)
    flow_field = centred(arg_keys[0], (NX, NY, M), 16.0, 96.0, ((0, 16), (1, 4), (2, 4)))
    left_x = centred(arg_keys[1], (NX, R), (NX * NX // 4) ** -0.5, 0.0234375, ((0, 16),))
    last_x = centred(arg_keys[2], (NX, R), NX ** -0.5, 0.25, ((0, 16),))
    last_y = centred(arg_keys[3], (NY, R), (NY * 4096) ** -0.5, 0.005859375, ((0, 4),))
    right_y = centred(arg_keys[4], (NY, L), NY ** -0.5, 0.375, ((0, 4),))
    right_m = centred(arg_keys[5], (M, L), M ** -0.5, 0.125, ((0, 4),))
    last_m = centred(arg_keys[6], (M, L), M ** -0.5, 0.125, ((0, 4),))
    return {"flow_field": flow_field, "left_x": left_x, "last_x": last_x, "last_y": last_y, "right_y": right_y, "right_m": right_m, "last_m": last_m}


def reference(flow_field, left_x, last_x, last_y, right_y, right_m, last_m):
    highest = lax.Precision.HIGHEST
    blocks = 8
    x_size = NX // blocks
    field_blocks = flow_field.reshape(blocks, x_size, NY, M)
    left_blocks = left_x.reshape(blocks, x_size, R)
    last_blocks = last_x.reshape(blocks, x_size, R)
    y_factor = right_y.astype(jnp.float32)
    y_left = last_y.astype(jnp.float32)

    def block_step(totals, pieces):
        x_block, left_piece, last_piece = pieces
        flat_field = x_block.reshape(x_size * NY, M)
        first_terms = jnp.dot(flat_field.astype(jnp.float32), right_m.astype(jnp.float32), preferred_element_type=jnp.float32).reshape(x_size, NY, L)
        first_rows = jnp.sum(first_terms * y_factor[None], axis=1)
        last_terms = jnp.dot(flat_field.astype(jnp.float32), last_m.astype(jnp.float32), preferred_element_type=jnp.float32).reshape(x_size, NY * L)
        middle_part = jnp.dot(left_piece.astype(jnp.float32).T, last_terms, precision=highest)
        khatri = (last_piece.astype(jnp.float32)[:, None, :] * y_left[None]).astype(jnp.bfloat16)
        khatri = khatri.reshape(x_size * NY, R)
        last_part = jnp.dot(khatri.T.astype(jnp.float32), flat_field.astype(jnp.float32), preferred_element_type=jnp.float32)
        return ((totals[0] + middle_part, totals[1] + last_part), first_rows)
    start = (jnp.zeros((R, NY * L), jnp.float32), jnp.zeros((R, M), jnp.float32))
    (middle_sum, core_last), first_rows = lax.scan(block_step, start, (field_blocks, left_blocks, last_blocks))
    first_rows = first_rows.reshape(NX, L)
    first_gram = jnp.dot(left_x.astype(jnp.float32).T, first_rows, precision=highest)
    gram_first = jnp.dot(first_gram, first_gram.T, precision=highest)
    core_first = jnp.linalg.solve(gram_first, jnp.dot(first_gram, first_rows.T, precision=highest)).T
    last_gram = jnp.dot(core_last, last_m.astype(jnp.float32), precision=highest)
    gram_last = jnp.dot(last_gram, last_gram.T, precision=highest)
    pinv_last = jnp.linalg.solve(gram_last, last_gram).T
    core_middle = jnp.dot(middle_sum.reshape(R * NY, L), pinv_last, precision=highest).reshape(R, NY, R)
    return (core_first, core_middle, core_last)
```

```python
import functools

import jax
import jax.numpy as jnp
from jax import lax
from jax.experimental import pallas as pl
from jax.experimental.pallas import tpu as pltpu
from jax.sharding import PartitionSpec as P

HIGHEST = lax.Precision.HIGHEST
NT = (((1,), (1,)), ((), ()))


def dot_nt(left, right, precision=HIGHEST):
    return lax.dot_general(
        left, right, NT, precision=precision, preferred_element_type=jnp.float32
    )


def split_dot(left, right):
    high = right.astype(jnp.bfloat16)
    low = (right - high.astype(jnp.float32)).astype(jnp.bfloat16)
    return jnp.dot(left, high, preferred_element_type=jnp.float32) + jnp.dot(
        left, low, preferred_element_type=jnp.float32
    )


def row_order(size):
    p = lax.broadcasted_iota(jnp.int32, (size, size), 0)
    rest, x, zl, core, zh = p & 1, (p >> 1) & 3, (p >> 3) & 1, (p >> 4) & 1, p >> 5
    a = (x << 5) + (zh << 3) + (zl << 2) + (core << 1) + rest
    lane = lax.broadcasted_iota(jnp.int32, (size, size), 1)
    return jnp.where(lane == a, 1.0, 0.0).astype(jnp.bfloat16)


def sweep_steps(mat, first, last):
    size = mat.shape[0]
    lane = lax.broadcasted_iota(jnp.int32, (size, size), 1)
    sub = lax.broadcasted_iota(jnp.int32, (size, size), 0)

    def step(k, carry):
        now = mat[...]
        row = mat[pl.ds(k, 1), :]
        here = lane == k
        col = jnp.sum(jnp.where(here, now, 0.0), axis=1, keepdims=True)
        pivot = jnp.sum(jnp.where(lane[:1] == k, row, 0.0), axis=1, keepdims=True)
        inv = 1.0 / pivot
        row_new = jnp.where(lane[:1] == k, 1.0, row) * inv
        kept = jnp.where(here, 0.0, now)
        mat[...] = jnp.where(sub == k, row_new, kept - col * row_new)
        return carry

    lax.fori_loop(first, last, step, 0)


def exchange_kernel(
    t_ref, z_ref, cl_ref, yf_ref, lx_ref, first_out, middle_out, last_out,
    z0, zs, z1, z1s, z2, z2s, zfull, qall, mat,
    c1, c1s, c2, cfull,
    y0, y0s, y1, y1s, y2,
    lxall, t0, ts, t1, t1s, t2, yp, t3, y3, y4, mm, obuf,
    send_sems, recv_sems,
):
    gx, gy, gz = lax.axis_index("gx"), lax.axis_index("gy"), lax.axis_index("gz")
    x, zh = gx // 4, gx % 4
    y = gy
    zl, core = gz // 2, gz % 2
    pos_xy = x * 4 + y
    pos_z = zh * 2 + zl
    pos_g = zl * 4 + x
    count = [0]

    def at(x_=None, y_=None, zh_=None, zl_=None, core_=None):
        x_ = x if x_ is None else x_
        y_ = y if y_ is None else y_
        zh_ = zh if zh_ is None else zh_
        zl_ = zl if zl_ is None else zl_
        core_ = core if core_ is None else core_
        return (x_ * 4 + zh_, y_, zl_ * 2 + core_)

    def send(src, dst, device):
        n = count[0]
        count[0] += 1
        copy = pltpu.make_async_remote_copy(
            src_ref=src, dst_ref=dst, send_sem=send_sems.at[n], recv_sem=recv_sems.at[n],
            device_id=device, device_id_type=pl.DeviceIdType.MESH,
        )
        copy.start()
        started.append(copy)
        return copy

    started = []

    def peer_xy(d):
        q = (pos_xy + d) % 16
        return q, at(x_=q // 4, y_=q % 4)

    def peer_z(d):
        q = (pos_z + d) % 8
        return q, at(zh_=q // 2, zl_=q % 2)

    def peer_g(d):
        q = (pos_g + d) % 8
        return q, at(zl_=q // 4, x_=q % 4)

    other_core = at(core_=1 - core)
    other_zl = at(zl_=1 - zl)

    barrier = pltpu.get_barrier_semaphore()
    greeted = [peer_xy(d)[1] for d in range(1, 16)] + [peer_z(d)[1] for d in range(1, 8)]
    greeted += [other_core]
    greeted += [at(zl_=1 - zl, x_=(x + d) % 4) for d in range(1, 4)]
    for device in greeted:
        pl.semaphore_signal(
            barrier, inc=1, device_id=device, device_id_type=pl.DeviceIdType.MESH
        )
    pl.semaphore_wait(barrier, len(greeted))

    z_core = send(z_ref.at[1 - core], z0, other_core)
    y_core = send(yf_ref, y0, other_core)
    t_core = {}
    for half in (1, 0):
        for d in (1, 2, 3, 0):
            j0 = pl.multiple_of(((zl + half) % 2) * 32 + ((x + d) % 4) * 8, 8)
            t_core[half, d] = send(
                t_ref.at[:, pl.ds(j0, 8), pl.ds(128, 128)], t0.at[half * 4 + d], other_core
            )
    lx_x = [send(lx_ref, lxall.at[x], at(x_=(x + d) % 4)) for d in range(1, 4)]
    lxall[x] = lx_ref[...]

    z_core.wait_recv()
    zs[...] = z_ref[core] + z0[...]
    z_xy = []
    for d in range(1, 16):
        q, device = peer_xy(d)
        z_xy.append(send(zs.at[pl.ds(pl.multiple_of(q * 8, 8), 8)], z1.at[d], device))
    c_xy = []
    for d in range(1, 16):
        q, device = peer_xy(d)
        c_xy.append(send(cl_ref.at[pl.ds(pl.multiple_of(q * 8, 8), 8)], c1.at[d], device))
    own_xy = pl.ds(pl.multiple_of(pos_xy * 8, 8), 8)

    def t_sum(half, d):
        t_core[half, d].wait_recv()
        j0 = pl.multiple_of(((zl + half) % 2) * 32 + ((x + d) % 4) * 8, 8)
        mine = t_ref[:, pl.ds(j0, 8), 0:128]
        ts[half * 4 + d] = (mine + t0[half * 4 + d]).reshape(256, 128)

    t_zl = {}
    for d in (1, 2):
        t_sum(1, d)
        t_zl[d] = send(ts.at[4 + d], t1.at[d], other_zl)
    y_core.wait_recv()
    y0s[...] = yf_ref[...] + y0[...]
    for d in (3, 0):
        t_sum(1, d)
    for d in (1, 2, 3, 0):
        t_sum(0, d)

    for copy in z_xy:
        copy.wait_recv()
    total = zs[own_xy]
    for d in range(1, 16):
        total = total + z1[d]
    z1s[...] = total
    z_z = []
    for d in range(1, 8):
        z_z.append(send(z1s, z2.at[d], peer_z(d)[1]))
    y_zl = send(y0s, y1, other_zl)
    for d in (3, 0):
        t_zl[d] = send(ts.at[4 + d], t1.at[d], other_zl)

    for copy in c_xy:
        copy.wait_recv()
    total = cl_ref[own_xy]
    for d in range(1, 16):
        total = total + c1[d]
    c1s[...] = total
    t_x = {}

    def t_forward(d):
        t_zl[d].wait_recv()
        t1s[d] = ts[d] + t1[d]
        if d:
            t_x[d] = send(
                t1s.at[d],
                t2.at[pl.ds(pl.multiple_of(x * 256, 256), 256)],
                at(x_=(x + d) % 4),
            )
        else:
            t2[pl.ds(pl.multiple_of(x * 256, 256), 256), :] = t1s[d]

    for d in (1, 2):
        t_forward(d)

    for copy in z_z:
        copy.wait_recv()
    total = z1s[...]
    for d in range(1, 8):
        total = total + z2[d]
    z2s[...] = total
    z_all = []
    for d in range(1, 16):
        z_all.append(send(z2s, zfull.at[own_xy], peer_xy(d)[1]))
    zfull[own_xy] = total
    c_z = [send(c1s, c2.at[d], at(zh_=(zh + d) % 4)) for d in range(1, 4)]
    y_zl.wait_recv()
    y1s[...] = y0s[...] + y1[...]
    y_y = [send(y1s, y2.at[d], at(y_=(y + d) % 4)) for d in range(1, 4)]
    for d in (3, 0):
        t_forward(d)
    for copy in lx_x:
        copy.wait_recv()
    left = dot_nt(
        row_order(128), lxall[...].reshape(128, 128).astype(jnp.bfloat16), None
    ).astype(jnp.bfloat16)

    for copy in z_all:
        copy.wait_recv()
    mat[...] = dot_nt(zfull[...], zfull[...])

    sweep_steps(mat, 0, 32)

    for copy in c_z:
        copy.wait_recv()
    total = c1s[...]
    for d in range(1, 4):
        total = total + c2[d]
    cfull[own_xy] = total
    c_all = []
    for d in range(1, 16):
        c_all.append(send(cfull.at[own_xy], cfull.at[own_xy], peer_xy(d)[1]))
    for copy in t_x.values():
        copy.wait_recv()
    for j in range(8):
        rows = pl.ds(j, 128, stride=8)
        yp[rows, :] = split_dot(left, t2[rows, :])
    t_zh = []
    for d in range(1, 4):
        q = (zh + d) % 4
        t_zh.append(
            send(yp.at[pl.ds(pl.multiple_of(q * 256, 256), 256)], t3.at[d], at(zh_=q))
        )

    sweep_steps(mat, 32, 128)

    inverse = mat[...]
    qall[core] = jnp.dot(
        inverse, zfull[...], precision=HIGHEST, preferred_element_type=jnp.float32
    )
    q_core = send(qall.at[core], qall.at[core], other_core)

    for copy in t_zh:
        copy.wait_recv()
    total = yp[pl.ds(pl.multiple_of(zh * 256, 256), 256), :]
    for d in range(1, 4):
        total = total + t3[d]
    y3[...] = total
    m_core = send(
        y3.at[pl.ds(pl.multiple_of((1 - core) * 128, 128), 128)], y4.at[core], other_core
    )
    y4[core] = y3[pl.ds(pl.multiple_of(core * 128, 128), 128), :]
    for copy in y_y:
        copy.wait_recv()
    total = y1s[...]
    for d in range(1, 4):
        total = total + y2[d]
    q_core.wait_recv()
    m_core.wait_recv()
    mixed = dot_nt(y4[0], qall[1, :, 0:128]) + dot_nt(y4[1], qall[1, :, 128:256])
    mm[...] = mixed.reshape(16, 8, 128)
    m_all = []
    own_j = pl.ds(pl.multiple_of(pos_g * 8, 8), 8)
    for d in range(1, 8):
        q, device = peer_g(d)
        m_all.append(send(mm.at[pl.ds(q * 2, 2)], obuf.at[:, own_j, :], device))
    obuf[:, own_j, :] = mm[pl.ds(pos_g * 2, 2)]
    first_out[...] = dot_nt(total, qall[0])
    for copy in c_all:
        copy.wait_recv()
    last_out[...] = cfull[...]
    for copy in m_all:
        copy.wait_recv()
    middle_out[...] = obuf[...]
    for copy in started:
        copy.wait_send()


COPIES = 1 + 1 + 8 + 3 + 15 + 15 + 4 + 7 + 1 + 3 + 15 + 3 + 3 + 15 + 3 + 1 + 1 + 7


def exchange(t_part, z_part, cl_part, yf_part, left_wide):
    f32 = jnp.float32
    shapes = [
        (128, 256), (128, 256), (16, 8, 256), (8, 256), (8, 8, 256), (8, 256), (128, 256),
        (2, 128, 256), (128, 128),
        (16, 8, 512), (8, 512), (4, 8, 512), (128, 512),
        (32, 256), (32, 256), (32, 256), (32, 256), (4, 32, 256),
        (4, 32, 128), (8, 32, 8, 128), (8, 256, 128), (4, 256, 128), (4, 256, 128),
        (1024, 128), (1024, 128), (4, 256, 128), (256, 128), (2, 128, 128),
        (16, 8, 128), (2, 64, 128),
    ]
    vmem = pl.BlockSpec(memory_space=pltpu.VMEM)
    return pl.pallas_call(
        exchange_kernel,
        out_shape=(
            jax.ShapeDtypeStruct((32, 128), f32),
            jax.ShapeDtypeStruct((2, 64, 128), f32),
            jax.ShapeDtypeStruct((128, 512), f32),
        ),
        in_specs=[vmem] * 5,
        out_specs=(vmem,) * 3,
        scratch_shapes=[pltpu.VMEM(shape, f32) for shape in shapes]
        + [pltpu.SemaphoreType.DMA((COPIES,)), pltpu.SemaphoreType.DMA((COPIES,))],
        compiler_params=pltpu.CompilerParams(
            collective_id=0, has_side_effects=True, vmem_limit_bytes=32 * 1024 * 1024
        ),
        name="exchange",
    )(t_part, z_part, cl_part, yf_part, left_wide)


def per_device(flow_field, left_x, last_x, last_y, right_y, right_m, last_m):
    x_cells, y_cells, m_cells = flow_field.shape
    rank_cols = left_x.shape[1]
    sketch_cols = right_m.shape[1]
    core = lax.axis_index("gz") % 2
    flat_field = flow_field.reshape(x_cells * y_cells, m_cells)
    first_terms = jnp.dot(flat_field, right_m, preferred_element_type=jnp.float32).reshape(
        x_cells, y_cells, sketch_cols
    )
    first_part = jnp.sum(first_terms * right_y.astype(jnp.float32)[None], axis=1)
    left_wide = left_x.astype(jnp.float32)
    z_first = jnp.dot(left_wide.T, first_part, precision=HIGHEST)
    khatri = (last_x.astype(jnp.float32)[:, None, :] * last_y.astype(jnp.float32)[None]).astype(
        jnp.bfloat16
    )
    khatri = khatri.reshape(x_cells * y_cells, rank_cols)
    last_part = jnp.dot(khatri.T, flat_field, preferred_element_type=jnp.float32)
    z_last = jnp.dot(last_part, last_m.astype(jnp.float32), precision=HIGHEST)
    z_part = jnp.stack([z_first, z_last])
    half = sketch_cols // 2
    own_m = jnp.where(core == 0, last_m[:, :half], last_m[:, half:])
    other_m = jnp.where(core == 0, last_m[:, half:], last_m[:, :half])
    own_first = jnp.concatenate([own_m, other_m], axis=1)
    t_part = jnp.dot(flat_field, own_first, preferred_element_type=jnp.float32).reshape(
        x_cells, y_cells, sketch_cols
    )
    return exchange(t_part, z_part, last_part, first_part, left_wide)


def solution(mesh):
    return jax.shard_map(
        per_device,
        mesh=mesh,
        in_specs=(
            P("gx", "gy", "gz"),
            P("gx", None),
            P("gx", None),
            P("gy", None),
            P("gy", None),
            P("gz", None),
            P("gz", None),
        ),
        out_specs=(P("gx", None), P(("gx", "gz"), "gy", None), P(None, "gz")),
        check_vma=False,
    )
```

```python
import jax
import jax.numpy as jnp
from jax import lax
from jax.experimental import pallas as pl
from jax.experimental.pallas import tpu as pltpu
from jax.sharding import PartitionSpec as P

HIGHEST = lax.Precision.HIGHEST
NT = (((1,), (1,)), ((), ()))
TN = (((0,), (0,)), ((), ()))
CELLS = 4


def dot_nt(left, right, precision=HIGHEST):
    return lax.dot_general(
        left, right, NT, precision=precision, preferred_element_type=jnp.float32
    )


def split_dot(left, right):
    high = right.astype(jnp.bfloat16)
    low = (right - high.astype(jnp.float32)).astype(jnp.bfloat16)
    return jnp.dot(left, high, preferred_element_type=jnp.float32) + jnp.dot(
        left, low, preferred_element_type=jnp.float32
    )


def three_parts(value):
    high = value.astype(jnp.bfloat16)
    rest = value - high.astype(jnp.float32)
    middle = rest.astype(jnp.bfloat16)
    low = (rest - middle.astype(jnp.float32)).astype(jnp.bfloat16)
    return high, middle, low


def dot_tn(left, right):
    return lax.dot_general(left, right, TN, preferred_element_type=jnp.float32)


def row_order(size):
    p = lax.broadcasted_iota(jnp.int32, (size, size), 0)
    rest, x, zl, core, zh = p & 1, (p >> 1) & 3, (p >> 3) & 1, (p >> 4) & 1, p >> 5
    a = (x << 5) + (zh << 3) + (zl << 2) + (core << 1) + rest
    lane = lax.broadcasted_iota(jnp.int32, (size, size), 1)
    return jnp.where(lane == a, 1.0, 0.0).astype(jnp.bfloat16)


def sweep_steps(mat, first, last):
    size = mat.shape[0]
    lane = lax.broadcasted_iota(jnp.int32, (size, size), 1)
    sub = lax.broadcasted_iota(jnp.int32, (size, size), 0)

    def step(k, carry):
        now = mat[...]
        row = mat[pl.ds(k, 1), :]
        here = lane == k
        col = jnp.sum(jnp.where(here, now, 0.0), axis=1, keepdims=True)
        pivot = jnp.sum(jnp.where(lane[:1] == k, row, 0.0), axis=1, keepdims=True)
        inv = 1.0 / pivot
        row_new = jnp.where(lane[:1] == k, 1.0, row) * inv
        kept = jnp.where(here, 0.0, now)
        mat[...] = jnp.where(sub == k, row_new, kept - col * row_new)
        return carry

    lax.fori_loop(first, last, step, 0)


def exchange_kernel(
    field_hbm, left_x_hbm, last_x_hbm, last_y_hbm, right_y_hbm, right_m_hbm, last_m_hbm,
    first_out, middle_out, last_out,
    field, left_x, last_x, last_y, right_y, right_m, last_m, kh,
    t_ref, z_ref, cl_ref, yf_ref, lx_ref,
    z0, zs, z1, z1s, z2, z2s, zfull, qall, mat,
    c1, c1s, c2, cfull,
    y0, y0s, y1, y1s, y2,
    lxall, t0, ts, t1, t1s, t2, yp, t3, y3, y4, mm, obuf,
    send_sems, recv_sems, load_sems,
):
    gx, gy, gz = lax.axis_index("gx"), lax.axis_index("gy"), lax.axis_index("gz")
    x, zh = gx // 4, gx % 4
    y = gy
    zl, core = gz // 2, gz % 2
    pos_xy = x * 4 + y
    pos_z = zh * 2 + zl
    pos_g = zl * 4 + x
    count = [0]

    def at(x_=None, y_=None, zh_=None, zl_=None, core_=None):
        x_ = x if x_ is None else x_
        y_ = y if y_ is None else y_
        zh_ = zh if zh_ is None else zh_
        zl_ = zl if zl_ is None else zl_
        core_ = core if core_ is None else core_
        return (x_ * 4 + zh_, y_, zl_ * 2 + core_)

    def send(src, dst, device):
        n = count[0]
        count[0] += 1
        copy = pltpu.make_async_remote_copy(
            src_ref=src, dst_ref=dst, send_sem=send_sems.at[n], recv_sem=recv_sems.at[n],
            device_id=device, device_id_type=pl.DeviceIdType.MESH,
        )
        copy.start()
        started.append(copy)
        return copy

    started = []

    def peer_xy(d):
        q = (pos_xy + d) % 16
        return q, at(x_=q // 4, y_=q % 4)

    def peer_z(d):
        q = (pos_z + d) % 8
        return q, at(zh_=q // 2, zl_=q % 2)

    def peer_g(d):
        q = (pos_g + d) % 8
        return q, at(zl_=q // 4, x_=q % 4)

    other_core = at(core_=1 - core)
    other_zl = at(zl_=1 - zl)

    barrier = pltpu.get_barrier_semaphore()
    greeted = [peer_xy(d)[1] for d in range(1, 16)] + [peer_z(d)[1] for d in range(1, 8)]
    greeted += [other_core]
    greeted += [at(zl_=1 - zl, x_=(x + d) % 4) for d in range(1, 4)]
    for device in greeted:
        pl.semaphore_signal(
            barrier, inc=1, device_id=device, device_id_type=pl.DeviceIdType.MESH
        )
    loads = [
        pltpu.make_async_copy(src, dst, load_sems.at[n])
        for n, (src, dst) in enumerate(
            (
                (last_x_hbm, last_x), (last_y_hbm, last_y), (right_y_hbm, right_y),
                (left_x_hbm, left_x), (field_hbm, field), (right_m_hbm, right_m),
                (last_m_hbm, last_m),
            )
        )
    ]
    for copy in loads:
        copy.start()
    for copy in loads[:4]:
        copy.wait()
    lx_ref[...] = left_x[...].astype(jnp.float32)
    y_cells = last_y.shape[0]
    last_x_wide = last_x[...].astype(jnp.float32)
    last_y_wide = last_y[...].astype(jnp.float32)
    for i in range(last_x.shape[0]):
        kh[i * y_cells : (i + 1) * y_cells] = (
            last_x_wide[i : i + 1] * last_y_wide
        ).astype(jnp.bfloat16)
    for copy in loads[4:]:
        copy.wait()
    cl_ref[...] = dot_tn(kh[...], field[...])
    weights = right_y[...].astype(jnp.float32)[None]
    for i in range(0, left_x.shape[0], CELLS):
        terms = jnp.dot(
            field[i * y_cells : (i + CELLS) * y_cells], right_m[...],
            preferred_element_type=jnp.float32,
        )
        yf_ref[i : i + CELLS] = jnp.sum(
            terms.reshape(CELLS, y_cells, terms.shape[1]) * weights, axis=1
        )
    z_ref[0] = sum(dot_tn(left_x[...], part) for part in three_parts(yf_ref[...]))
    z_ref[1] = sum(
        jnp.dot(part, last_m[...], preferred_element_type=jnp.float32)
        for part in three_parts(cl_ref[...])
    )
    pl.semaphore_wait(barrier, len(greeted))

    z_core = send(z_ref.at[1 - core], z0, other_core)
    y_core = send(yf_ref, y0, other_core)
    for i in range(0, left_x.shape[0], CELLS):
        terms = jnp.dot(
            field[i * y_cells : (i + CELLS) * y_cells], last_m[...],
            preferred_element_type=jnp.float32,
        ).reshape(CELLS, y_cells, 256)
        for c in range(2):
            t_ref[c, i : i + CELLS] = terms[:, :, c * 128 : (c + 1) * 128]
    t_core = {}
    for half in (1, 0):
        for d in (1, 2, 3, 0):
            j0 = pl.multiple_of(((zl + half) % 2) * 32 + ((x + d) % 4) * 8, 8)
            t_core[half, d] = send(
                t_ref.at[1 - core, :, pl.ds(j0, 8)], t0.at[half * 4 + d], other_core
            )
    lx_x = [send(lx_ref, lxall.at[x], at(x_=(x + d) % 4)) for d in range(1, 4)]
    lxall[x] = lx_ref[...]

    z_core.wait_recv()
    zs[...] = z_ref[core] + z0[...]
    z_xy = []
    for d in range(1, 16):
        q, device = peer_xy(d)
        z_xy.append(send(zs.at[pl.ds(pl.multiple_of(q * 8, 8), 8)], z1.at[d], device))
    c_xy = []
    for d in range(1, 16):
        q, device = peer_xy(d)
        c_xy.append(send(cl_ref.at[pl.ds(pl.multiple_of(q * 8, 8), 8)], c1.at[d], device))
    own_xy = pl.ds(pl.multiple_of(pos_xy * 8, 8), 8)

    def t_sum(half, d):
        t_core[half, d].wait_recv()
        j0 = pl.multiple_of(((zl + half) % 2) * 32 + ((x + d) % 4) * 8, 8)
        mine = t_ref[core, :, pl.ds(j0, 8), :]
        ts[half * 4 + d] = (mine + t0[half * 4 + d]).reshape(256, 128)

    t_zl = {}
    for d in (1, 2):
        t_sum(1, d)
        t_zl[d] = send(ts.at[4 + d], t1.at[d], other_zl)
    y_core.wait_recv()
    y0s[...] = yf_ref[...] + y0[...]
    for d in (3, 0):
        t_sum(1, d)
    for d in (1, 2, 3, 0):
        t_sum(0, d)

    for copy in z_xy:
        copy.wait_recv()
    total = zs[own_xy]
    for d in range(1, 16):
        total = total + z1[d]
    z1s[...] = total
    z_z = []
    for d in range(1, 8):
        z_z.append(send(z1s, z2.at[d], peer_z(d)[1]))
    y_zl = send(y0s, y1, other_zl)
    for d in (3, 0):
        t_zl[d] = send(ts.at[4 + d], t1.at[d], other_zl)

    for copy in c_xy:
        copy.wait_recv()
    total = cl_ref[own_xy]
    for d in range(1, 16):
        total = total + c1[d]
    c1s[...] = total
    t_x = {}

    def t_forward(d):
        t_zl[d].wait_recv()
        t1s[d] = ts[d] + t1[d]
        if d:
            t_x[d] = send(
                t1s.at[d],
                t2.at[pl.ds(pl.multiple_of(x * 256, 256), 256)],
                at(x_=(x + d) % 4),
            )
        else:
            t2[pl.ds(pl.multiple_of(x * 256, 256), 256), :] = t1s[d]

    for d in (1, 2):
        t_forward(d)

    for copy in z_z:
        copy.wait_recv()
    total = z1s[...]
    for d in range(1, 8):
        total = total + z2[d]
    z2s[...] = total
    z_all = []
    for d in range(1, 16):
        z_all.append(send(z2s, zfull.at[own_xy], peer_xy(d)[1]))
    zfull[own_xy] = total
    c_z = [send(c1s, c2.at[d], at(zh_=(zh + d) % 4)) for d in range(1, 4)]
    y_zl.wait_recv()
    y1s[...] = y0s[...] + y1[...]
    y_y = [send(y1s, y2.at[d], at(y_=(y + d) % 4)) for d in range(1, 4)]
    for d in (3, 0):
        t_forward(d)
    for copy in lx_x:
        copy.wait_recv()
    left = dot_nt(
        row_order(128), lxall[...].reshape(128, 128).astype(jnp.bfloat16), None
    ).astype(jnp.bfloat16)

    for copy in z_all:
        copy.wait_recv()
    mat[...] = dot_nt(zfull[...], zfull[...])

    sweep_steps(mat, 0, 32)

    for copy in c_z:
        copy.wait_recv()
    total = c1s[...]
    for d in range(1, 4):
        total = total + c2[d]
    cfull[own_xy] = total
    c_all = []
    for d in range(1, 16):
        c_all.append(send(cfull.at[own_xy], cfull.at[own_xy], peer_xy(d)[1]))
    for copy in t_x.values():
        copy.wait_recv()
    for j in range(8):
        rows = pl.ds(j, 128, stride=8)
        yp[rows, :] = split_dot(left, t2[rows, :])
    t_zh = []
    for d in range(1, 4):
        q = (zh + d) % 4
        t_zh.append(
            send(yp.at[pl.ds(pl.multiple_of(q * 256, 256), 256)], t3.at[d], at(zh_=q))
        )

    sweep_steps(mat, 32, 128)

    inverse = mat[...]
    qall[core] = jnp.dot(
        inverse, zfull[...], precision=HIGHEST, preferred_element_type=jnp.float32
    )
    q_core = send(qall.at[core], qall.at[core], other_core)

    for copy in t_zh:
        copy.wait_recv()
    total = yp[pl.ds(pl.multiple_of(zh * 256, 256), 256), :]
    for d in range(1, 4):
        total = total + t3[d]
    y3[...] = total
    m_core = send(
        y3.at[pl.ds(pl.multiple_of((1 - core) * 128, 128), 128)], y4.at[core], other_core
    )
    y4[core] = y3[pl.ds(pl.multiple_of(core * 128, 128), 128), :]
    for copy in y_y:
        copy.wait_recv()
    total = y1s[...]
    for d in range(1, 4):
        total = total + y2[d]
    q_core.wait_recv()
    m_core.wait_recv()
    mixed = dot_nt(y4[0], qall[1, :, 0:128]) + dot_nt(y4[1], qall[1, :, 128:256])
    mm[...] = mixed.reshape(16, 8, 128)
    m_all = []
    own_j = pl.ds(pl.multiple_of(pos_g * 8, 8), 8)
    for d in range(1, 8):
        q, device = peer_g(d)
        m_all.append(send(mm.at[pl.ds(q * 2, 2)], obuf.at[:, own_j, :], device))
    obuf[:, own_j, :] = mm[pl.ds(pos_g * 2, 2)]
    first_out[...] = dot_nt(total, qall[0])
    for copy in c_all:
        copy.wait_recv()
    last_out[...] = cfull[...]
    for copy in m_all:
        copy.wait_recv()
    middle_out[...] = obuf[...]
    for copy in started:
        copy.wait_send()


COPIES = 1 + 1 + 8 + 3 + 15 + 15 + 4 + 7 + 1 + 3 + 15 + 3 + 3 + 15 + 3 + 1 + 1 + 7


def per_device(flow_field, left_x, last_x, last_y, right_y, right_m, last_m):
    f32 = jnp.float32
    flat_field = flow_field.reshape(-1, flow_field.shape[2])
    inputs = (flat_field, left_x, last_x, last_y, right_y, right_m, last_m)
    shapes = [
        (2, 32, 64, 128), (2, 128, 256), (128, 512), (32, 256), (32, 128),
        (128, 256), (128, 256), (16, 8, 256), (8, 256), (8, 8, 256), (8, 256), (128, 256),
        (2, 128, 256), (128, 128),
        (16, 8, 512), (8, 512), (4, 8, 512), (128, 512),
        (32, 256), (32, 256), (32, 256), (32, 256), (4, 32, 256),
        (4, 32, 128), (8, 32, 8, 128), (8, 256, 128), (4, 256, 128), (4, 256, 128),
        (1024, 128), (1024, 128), (4, 256, 128), (256, 128), (2, 128, 128),
        (16, 8, 128), (2, 64, 128),
    ]
    vmem = pl.BlockSpec(memory_space=pltpu.VMEM)
    return pl.pallas_call(
        exchange_kernel,
        out_shape=(
            jax.ShapeDtypeStruct((32, 128), f32),
            jax.ShapeDtypeStruct((2, 64, 128), f32),
            jax.ShapeDtypeStruct((128, 512), f32),
        ),
        in_specs=[pl.BlockSpec(memory_space=pl.ANY)] * 7,
        out_specs=(vmem,) * 3,
        scratch_shapes=[pltpu.VMEM(array.shape, jnp.bfloat16) for array in inputs]
        + [pltpu.VMEM((2048, 128), jnp.bfloat16)]
        + [pltpu.VMEM(shape, f32) for shape in shapes]
        + [pltpu.SemaphoreType.DMA((count,)) for count in (COPIES, COPIES, 7)],
        compiler_params=pltpu.CompilerParams(
            collective_id=0, has_side_effects=True, vmem_limit_bytes=32 * 1024 * 1024
        ),
        name="exchange",
    )(*inputs)


def solution(mesh):
    return jax.shard_map(
        per_device,
        mesh=mesh,
        in_specs=(
            P("gx", "gy", "gz"),
            P("gx", None),
            P("gx", None),
            P("gy", None),
            P("gy", None),
            P("gz", None),
            P("gz", None),
        ),
        out_specs=(P("gx", None), P(("gx", "gz"), "gy", None), P(None, "gz")),
        check_vma=False,
    )
```

```python
import jax
import jax.numpy as jnp
from jax import lax
from jax.experimental import pallas as pl
from jax.experimental.pallas import tpu as pltpu
from jax.sharding import PartitionSpec as P

HIGHEST = lax.Precision.HIGHEST
NT = (((1,), (1,)), ((), ()))
TN = (((0,), (0,)), ((), ()))
CELLS = 4


def dot_nt(left, right, precision=HIGHEST):
    return lax.dot_general(
        left, right, NT, precision=precision, preferred_element_type=jnp.float32
    )


def split_dot(left, right):
    high = right.astype(jnp.bfloat16)
    low = (right - high.astype(jnp.float32)).astype(jnp.bfloat16)
    return jnp.dot(left, high, preferred_element_type=jnp.float32) + jnp.dot(
        left, low, preferred_element_type=jnp.float32
    )


def three_parts(value):
    high = value.astype(jnp.bfloat16)
    rest = value - high.astype(jnp.float32)
    middle = rest.astype(jnp.bfloat16)
    low = (rest - middle.astype(jnp.float32)).astype(jnp.bfloat16)
    return high, middle, low


def dot_tn(left, right):
    return lax.dot_general(left, right, TN, preferred_element_type=jnp.float32)


def row_order(size):
    p = lax.broadcasted_iota(jnp.int32, (size, size), 0)
    rest, x, zl, core, zh = p & 1, (p >> 1) & 3, (p >> 3) & 1, (p >> 4) & 1, p >> 5
    a = (x << 5) + (zh << 3) + (zl << 2) + (core << 1) + rest
    lane = lax.broadcasted_iota(jnp.int32, (size, size), 1)
    return jnp.where(lane == a, 1.0, 0.0).astype(jnp.bfloat16)


def sweep_steps(mat, first, last):
    size = mat.shape[0]
    lane = lax.broadcasted_iota(jnp.int32, (size, size), 1)
    sub = lax.broadcasted_iota(jnp.int32, (size, size), 0)

    def step(k, carry):
        now = mat[...]
        row = mat[pl.ds(k, 1), :]
        here = lane == k
        col = jnp.sum(jnp.where(here, now, 0.0), axis=1, keepdims=True)
        pivot = jnp.sum(jnp.where(lane[:1] == k, row, 0.0), axis=1, keepdims=True)
        inv = 1.0 / pivot
        row_new = jnp.where(lane[:1] == k, 1.0, row) * inv
        kept = jnp.where(here, 0.0, now)
        mat[...] = jnp.where(sub == k, row_new, kept - col * row_new)
        return carry

    lax.fori_loop(first, last, step, 0)


def exchange_kernel(
    field_hbm, left_x_hbm, last_x_hbm, last_y_hbm, right_y_hbm, right_m_hbm, last_m_hbm,
    first_out, middle_out, last_out,
    field, left_x, last_x, last_y, right_y, right_m, last_m, kh,
    t_ref, z_ref, cl_ref, yf_ref, lx_ref,
    z0, zs, z1, z1s, z2, z2s, zfull, qall, mat,
    c1, c1s, c2, cfull,
    y0, y0s, y1, y1s, y2,
    lxall, t0, ts, t1, t1s, t2, yp, t3, y3, y4, mm, obuf,
    send_sems, recv_sems, load_sems,
):
    gx, gy, gz = lax.axis_index("gx"), lax.axis_index("gy"), lax.axis_index("gz")
    x, zh = gx // 4, gx % 4
    y = gy
    zl, core = gz // 2, gz % 2
    pos_xy = x * 4 + y
    pos_z = zh * 2 + zl
    pos_g = zl * 4 + x
    count = [0]

    def at(x_=None, y_=None, zh_=None, zl_=None, core_=None):
        x_ = x if x_ is None else x_
        y_ = y if y_ is None else y_
        zh_ = zh if zh_ is None else zh_
        zl_ = zl if zl_ is None else zl_
        core_ = core if core_ is None else core_
        return (x_ * 4 + zh_, y_, zl_ * 2 + core_)

    def send(src, dst, device):
        n = count[0]
        count[0] += 1
        copy = pltpu.make_async_remote_copy(
            src_ref=src, dst_ref=dst, send_sem=send_sems.at[n], recv_sem=recv_sems.at[n],
            device_id=device, device_id_type=pl.DeviceIdType.MESH,
        )
        copy.start()
        started.append(copy)
        return copy

    started = []

    def peer_xy(d):
        q = (pos_xy + d) % 16
        return q, at(x_=q // 4, y_=q % 4)

    def peer_z(d):
        q = (pos_z + d) % 8
        return q, at(zh_=q // 2, zl_=q % 2)

    def peer_g(d):
        q = (pos_g + d) % 8
        return q, at(zl_=q // 4, x_=q % 4)

    other_core = at(core_=1 - core)
    other_zl = at(zl_=1 - zl)

    barrier = pltpu.get_barrier_semaphore()
    greeted = [peer_xy(d)[1] for d in range(1, 16)] + [peer_z(d)[1] for d in range(1, 8)]
    greeted += [other_core]
    greeted += [at(zl_=1 - zl, x_=(x + d) % 4) for d in range(1, 4)]
    for device in greeted:
        pl.semaphore_signal(
            barrier, inc=1, device_id=device, device_id_type=pl.DeviceIdType.MESH
        )
    loads = [
        pltpu.make_async_copy(src, dst, load_sems.at[n])
        for n, (src, dst) in enumerate(
            (
                (last_x_hbm, last_x), (last_y_hbm, last_y), (right_y_hbm, right_y),
                (left_x_hbm, left_x), (field_hbm, field), (right_m_hbm, right_m),
                (last_m_hbm, last_m),
            )
        )
    ]
    for copy in loads:
        copy.start()
    for copy in loads[:4]:
        copy.wait()
    lx_ref[...] = left_x[...].astype(jnp.float32)
    y_cells = last_y.shape[0]
    last_x_wide = last_x[...].astype(jnp.float32)
    last_y_wide = last_y[...].astype(jnp.float32)
    for i in range(last_x.shape[0]):
        kh[i * y_cells : (i + 1) * y_cells] = (
            last_x_wide[i : i + 1] * last_y_wide
        ).astype(jnp.bfloat16)
    for copy in loads[4:]:
        copy.wait()
    cl_ref[...] = dot_tn(kh[...], field[...])
    weights = right_y[...].astype(jnp.float32)[None]
    for i in range(0, left_x.shape[0], CELLS):
        terms = jnp.dot(
            field[i * y_cells : (i + CELLS) * y_cells], right_m[...],
            preferred_element_type=jnp.float32,
        )
        yf_ref[i : i + CELLS] = jnp.sum(
            terms.reshape(CELLS, y_cells, terms.shape[1]) * weights, axis=1
        )
    z_ref[0] = sum(dot_tn(left_x[...], part) for part in three_parts(yf_ref[...]))
    z_ref[1] = sum(
        jnp.dot(part, last_m[...], preferred_element_type=jnp.float32)
        for part in three_parts(cl_ref[...])
    )
    pl.semaphore_wait(barrier, len(greeted))

    z_core = send(z_ref.at[1 - core], z0, other_core)
    y_core = send(yf_ref, y0, other_core)
    for i in range(0, left_x.shape[0], CELLS):
        terms = jnp.dot(
            field[i * y_cells : (i + CELLS) * y_cells], last_m[...],
            preferred_element_type=jnp.float32,
        ).reshape(CELLS, y_cells, 256)
        for c in range(2):
            t_ref[c, i : i + CELLS] = terms[:, :, c * 128 : (c + 1) * 128]
    t_core = {}
    for half in (1, 0):
        for d in (1, 2, 3, 0):
            j0 = pl.multiple_of(((zl + half) % 2) * 32 + ((x + d) % 4) * 8, 8)
            t_core[half, d] = send(
                t_ref.at[1 - core, :, pl.ds(j0, 8)], t0.at[half * 4 + d], other_core
            )
    lx_x = [send(lx_ref, lxall.at[x], at(x_=(x + d) % 4)) for d in range(1, 4)]
    lxall[x] = lx_ref[...]

    z_core.wait_recv()
    zs[...] = z_ref[core] + z0[...]
    z_xy = []
    for d in range(1, 16):
        q, device = peer_xy(d)
        z_xy.append(send(zs.at[pl.ds(pl.multiple_of(q * 8, 8), 8)], z1.at[d], device))
    c_xy = []
    for d in range(1, 16):
        q, device = peer_xy(d)
        c_xy.append(send(cl_ref.at[pl.ds(pl.multiple_of(q * 8, 8), 8)], c1.at[d], device))
    own_xy = pl.ds(pl.multiple_of(pos_xy * 8, 8), 8)

    def t_sum(half, d):
        t_core[half, d].wait_recv()
        j0 = pl.multiple_of(((zl + half) % 2) * 32 + ((x + d) % 4) * 8, 8)
        mine = t_ref[core, :, pl.ds(j0, 8), :]
        ts[half * 4 + d] = (mine + t0[half * 4 + d]).reshape(256, 128)

    t_zl = {}
    for d in (1, 2):
        t_sum(1, d)
        t_zl[d] = send(ts.at[4 + d], t1.at[d], other_zl)
    y_core.wait_recv()
    y0s[...] = yf_ref[...] + y0[...]
    for d in (3, 0):
        t_sum(1, d)
    for d in (1, 2, 3, 0):
        t_sum(0, d)

    for copy in z_xy:
        copy.wait_recv()
    total = zs[own_xy]
    for d in range(1, 16):
        total = total + z1[d]
    z1s[...] = total
    z_z = []
    for d in range(1, 8):
        z_z.append(send(z1s, z2.at[d], peer_z(d)[1]))
    y_zl = send(y0s, y1, other_zl)
    for d in (3, 0):
        t_zl[d] = send(ts.at[4 + d], t1.at[d], other_zl)

    for copy in c_xy:
        copy.wait_recv()
    total = cl_ref[own_xy]
    for d in range(1, 16):
        total = total + c1[d]
    c1s[...] = total
    t_x = {}

    def t_forward(d):
        t_zl[d].wait_recv()
        t1s[d] = ts[d] + t1[d]
        if d:
            t_x[d] = send(
                t1s.at[d],
                t2.at[pl.ds(pl.multiple_of(x * 256, 256), 256)],
                at(x_=(x + d) % 4),
            )
        else:
            t2[pl.ds(pl.multiple_of(x * 256, 256), 256), :] = t1s[d]

    for d in (1, 2):
        t_forward(d)

    for copy in z_z:
        copy.wait_recv()
    total = z1s[...]
    for d in range(1, 8):
        total = total + z2[d]
    z2s[...] = total
    z_all = []
    for d in range(1, 16):
        z_all.append(send(z2s, zfull.at[own_xy], peer_xy(d)[1]))
    zfull[own_xy] = total
    c_z = [send(c1s, c2.at[d], at(zh_=(zh + d) % 4)) for d in range(1, 4)]
    y_zl.wait_recv()
    y1s[...] = y0s[...] + y1[...]
    y_y = [send(y1s, y2.at[d], at(y_=(y + d) % 4)) for d in range(1, 4)]
    for d in (3, 0):
        t_forward(d)
    for copy in lx_x:
        copy.wait_recv()
    left = dot_nt(
        row_order(128), lxall[...].reshape(128, 128).astype(jnp.bfloat16), None
    ).astype(jnp.bfloat16)

    for copy in z_all:
        copy.wait_recv()
    mat[...] = dot_nt(zfull[...], zfull[...])

    sweep_steps(mat, 0, 32)

    for copy in c_z:
        copy.wait_recv()
    total = c1s[...]
    for d in range(1, 4):
        total = total + c2[d]
    cfull[own_xy] = total
    c_all = []
    for d in range(1, 16):
        c_all.append(send(cfull.at[own_xy], cfull.at[own_xy], peer_xy(d)[1]))
    for copy in t_x.values():
        copy.wait_recv()
    for j in range(8):
        rows = pl.ds(j, 128, stride=8)
        yp[rows, :] = split_dot(left, t2[rows, :])
    t_zh = []
    for d in range(1, 4):
        q = (zh + d) % 4
        t_zh.append(
            send(yp.at[pl.ds(pl.multiple_of(q * 256, 256), 256)], t3.at[d], at(zh_=q))
        )

    sweep_steps(mat, 32, 128)

    inverse = mat[...]
    qall[core] = jnp.dot(
        inverse, zfull[...], precision=HIGHEST, preferred_element_type=jnp.float32
    )
    q_core = send(qall.at[core], qall.at[core], other_core)

    for copy in t_zh:
        copy.wait_recv()
    total = yp[pl.ds(pl.multiple_of(zh * 256, 256), 256), :]
    for d in range(1, 4):
        total = total + t3[d]
    y3[...] = total
    m_core = send(
        y3.at[pl.ds(pl.multiple_of((1 - core) * 128, 128), 128)], y4.at[core], other_core
    )
    y4[core] = y3[pl.ds(pl.multiple_of(core * 128, 128), 128), :]
    for copy in y_y:
        copy.wait_recv()
    total = y1s[...]
    for d in range(1, 4):
        total = total + y2[d]
    q_core.wait_recv()
    m_core.wait_recv()
    mixed = dot_nt(y4[0], qall[1, :, 0:128]) + dot_nt(y4[1], qall[1, :, 128:256])
    mm[...] = mixed.reshape(16, 8, 128)
    m_all = []
    own_j = pl.ds(pl.multiple_of(pos_g * 8, 8), 8)
    for d in range(1, 8):
        q, device = peer_g(d)
        m_all.append(send(mm.at[pl.ds(q * 2, 2)], obuf.at[:, own_j, :], device))
    obuf[:, own_j, :] = mm[pl.ds(pos_g * 2, 2)]
    first_out[...] = dot_nt(total, qall[0])
    for copy in c_all:
        copy.wait_recv()
    last_out[...] = cfull[...]
    for copy in m_all:
        copy.wait_recv()
    middle_out[...] = obuf[...]
    for copy in started:
        copy.wait_send()


COPIES = 1 + 1 + 8 + 3 + 15 + 15 + 4 + 7 + 1 + 3 + 15 + 3 + 3 + 15 + 3 + 1 + 1 + 7


def per_device(flow_field, left_x, last_x, last_y, right_y, right_m, last_m):
    f32 = jnp.float32
    flat_field = flow_field.reshape(-1, flow_field.shape[2])
    inputs = (flat_field, left_x, last_x, last_y, right_y, right_m, last_m)
    shapes = [
        (2, 32, 64, 128), (2, 128, 256), (128, 512), (32, 256), (32, 128),
        (128, 256), (128, 256), (16, 8, 256), (8, 256), (8, 8, 256), (8, 256), (128, 256),
        (2, 128, 256), (128, 128),
        (16, 8, 512), (8, 512), (4, 8, 512), (128, 512),
        (32, 256), (32, 256), (32, 256), (32, 256), (4, 32, 256),
        (4, 32, 128), (8, 32, 8, 128), (8, 256, 128), (4, 256, 128), (4, 256, 128),
        (1024, 128), (1024, 128), (4, 256, 128), (256, 128), (2, 128, 128),
        (16, 8, 128), (2, 64, 128),
    ]
    vmem = pl.BlockSpec(memory_space=pltpu.VMEM)
    return pl.pallas_call(
        exchange_kernel,
        out_shape=(
            jax.ShapeDtypeStruct((32, 128), f32),
            jax.ShapeDtypeStruct((2, 64, 128), f32),
            jax.ShapeDtypeStruct((128, 512), f32),
        ),
        in_specs=[pl.BlockSpec(memory_space=pl.ANY)] * 7,
        out_specs=(vmem,) * 3,
        scratch_shapes=[pltpu.VMEM(array.shape, jnp.bfloat16) for array in inputs]
        + [pltpu.VMEM((2048, 128), jnp.bfloat16)]
        + [pltpu.VMEM(shape, f32) for shape in shapes]
        + [pltpu.SemaphoreType.DMA((count,)) for count in (COPIES, COPIES, 7)],
        compiler_params=pltpu.CompilerParams(
            collective_id=0, has_side_effects=True, vmem_limit_bytes=67_043_328
        ),
        name="exchange",
    )(*inputs)


def solution(mesh):
    return jax.shard_map(
        per_device,
        mesh=mesh,
        in_specs=(
            P("gx", "gy", "gz"),
            P("gx", None),
            P("gx", None),
            P("gy", None),
            P("gy", None),
            P("gz", None),
            P("gz", None),
        ),
        out_specs=(P("gx", None), P(("gx", "gz"), "gy", None), P(None, "gz")),
        check_vma=False,
    )
```

```python
import jax
import jax.numpy as jnp
from jax import lax
from jax.experimental import pallas as pl
from jax.experimental.pallas import tpu as pltpu
from jax.sharding import PartitionSpec as P

HIGHEST = lax.Precision.HIGHEST
NT = (((1,), (1,)), ((), ()))
TN = (((0,), (0,)), ((), ()))
CELLS = 4


def dot_nt(left, right, precision=HIGHEST):
    return lax.dot_general(
        left, right, NT, precision=precision, preferred_element_type=jnp.float32
    )


def split_dot(left, right):
    high = right.astype(jnp.bfloat16)
    low = (right - high.astype(jnp.float32)).astype(jnp.bfloat16)
    return jnp.dot(left, high, preferred_element_type=jnp.float32) + jnp.dot(
        left, low, preferred_element_type=jnp.float32
    )


def three_parts(value):
    high = value.astype(jnp.bfloat16)
    rest = value - high.astype(jnp.float32)
    middle = rest.astype(jnp.bfloat16)
    low = (rest - middle.astype(jnp.float32)).astype(jnp.bfloat16)
    return high, middle, low


def dot_tn(left, right):
    return lax.dot_general(left, right, TN, preferred_element_type=jnp.float32)


def row_order(size):
    p = lax.broadcasted_iota(jnp.int32, (size, size), 0)
    rest, x, zl, core, zh = p & 1, (p >> 1) & 3, (p >> 3) & 1, (p >> 4) & 1, p >> 5
    a = (x << 5) + (zh << 3) + (zl << 2) + (core << 1) + rest
    lane = lax.broadcasted_iota(jnp.int32, (size, size), 1)
    return jnp.where(lane == a, 1.0, 0.0).astype(jnp.bfloat16)


def sweep_steps(mat, first, last):
    size = mat.shape[0]
    lane = lax.broadcasted_iota(jnp.int32, (size, size), 1)
    sub = lax.broadcasted_iota(jnp.int32, (size, size), 0)

    def step(n, carry):
        k = 2 * n
        now = mat[...]
        pair = mat[pl.ds(k, 2), :]
        row0, row1 = pair[0:1], pair[1:2]
        at0, at1 = lane == k, lane == k + 1
        here0, here1 = at0[:1], at1[:1]
        col0 = jnp.sum(jnp.where(at0, now, 0.0), axis=1, keepdims=True)
        col1 = jnp.sum(jnp.where(at1, now, 0.0), axis=1, keepdims=True)
        a = jnp.sum(jnp.where(here0, row0, 0.0), axis=1, keepdims=True)
        b = jnp.sum(jnp.where(here1, row0, 0.0), axis=1, keepdims=True)
        c = jnp.sum(jnp.where(here0, row1, 0.0), axis=1, keepdims=True)
        d = jnp.sum(jnp.where(here1, row1, 0.0), axis=1, keepdims=True)
        inv = 1.0 / a
        ratio = c * inv
        last_inv = 1.0 / (d - ratio * b)
        unit0 = jnp.where(here0, 1.0, jnp.where(here1, 0.0, row0))
        unit1 = jnp.where(here1, 1.0, jnp.where(here0, 0.0, row1))
        new1 = (unit1 - ratio * unit0) * last_inv
        new0 = (unit0 - b * new1) * inv
        kept = jnp.where(at0 | at1, 0.0, now)
        kept = kept - col0 * new0 - col1 * new1
        mat[...] = jnp.where(sub == k, new0, jnp.where(sub == k + 1, new1, kept))
        return carry

    lax.fori_loop(first // 2, last // 2, step, 0)


def exchange_kernel(
    field_hbm, left_x_hbm, last_x_hbm, last_y_hbm, right_y_hbm, right_m_hbm, last_m_hbm,
    first_out, middle_out, last_out,
    field, left_x, last_x, last_y, right_y, right_m, last_m, kh,
    t_ref, z_ref, cl_ref, yf_ref, lx_ref,
    z0, zs, z1, z1s, z2, z2s, zfull, qall, mat,
    c1, c1s, c2, cfull,
    y0, y0s, y1, y1s, y2,
    lxall, t0, ts, t1, t1s, t2, yp, t3, y3, y4, mm, obuf,
    send_sems, recv_sems, load_sems,
):
    gx, gy, gz = lax.axis_index("gx"), lax.axis_index("gy"), lax.axis_index("gz")
    x, zh = gx // 4, gx % 4
    y = gy
    zl, core = gz // 2, gz % 2
    pos_xy = x * 4 + y
    pos_z = zh * 2 + zl
    pos_g = zl * 4 + x
    count = [0]

    def at(x_=None, y_=None, zh_=None, zl_=None, core_=None):
        x_ = x if x_ is None else x_
        y_ = y if y_ is None else y_
        zh_ = zh if zh_ is None else zh_
        zl_ = zl if zl_ is None else zl_
        core_ = core if core_ is None else core_
        return (x_ * 4 + zh_, y_, zl_ * 2 + core_)

    def send(src, dst, device):
        n = count[0]
        count[0] += 1
        copy = pltpu.make_async_remote_copy(
            src_ref=src, dst_ref=dst, send_sem=send_sems.at[n], recv_sem=recv_sems.at[n],
            device_id=device, device_id_type=pl.DeviceIdType.MESH,
        )
        copy.start()
        started.append(copy)
        return copy

    started = []

    def peer_xy(d):
        q = (pos_xy + d) % 16
        return q, at(x_=q // 4, y_=q % 4)

    def peer_z(d):
        q = (pos_z + d) % 8
        return q, at(zh_=q // 2, zl_=q % 2)

    def peer_g(d):
        q = (pos_g + d) % 8
        return q, at(zl_=q // 4, x_=q % 4)

    other_core = at(core_=1 - core)
    other_zl = at(zl_=1 - zl)

    barrier = pltpu.get_barrier_semaphore()
    greeted = [peer_xy(d)[1] for d in range(1, 16)] + [peer_z(d)[1] for d in range(1, 8)]
    greeted += [other_core]
    greeted += [at(zl_=1 - zl, x_=(x + d) % 4) for d in range(1, 4)]
    for device in greeted:
        pl.semaphore_signal(
            barrier, inc=1, device_id=device, device_id_type=pl.DeviceIdType.MESH
        )
    loads = [
        pltpu.make_async_copy(src, dst, load_sems.at[n])
        for n, (src, dst) in enumerate(
            (
                (last_x_hbm, last_x), (last_y_hbm, last_y), (right_y_hbm, right_y),
                (left_x_hbm, left_x), (field_hbm, field), (right_m_hbm, right_m),
                (last_m_hbm, last_m),
            )
        )
    ]
    for copy in loads:
        copy.start()
    for copy in loads[:4]:
        copy.wait()
    lx_ref[...] = left_x[...].astype(jnp.float32)
    y_cells = last_y.shape[0]
    last_x_wide = last_x[...].astype(jnp.float32)
    last_y_wide = last_y[...].astype(jnp.float32)
    for i in range(last_x.shape[0]):
        kh[i * y_cells : (i + 1) * y_cells] = (
            last_x_wide[i : i + 1] * last_y_wide
        ).astype(jnp.bfloat16)
    for copy in loads[4:]:
        copy.wait()
    cl_ref[...] = dot_tn(kh[...], field[...])
    weights = right_y[...].astype(jnp.float32)[None]
    for i in range(0, left_x.shape[0], CELLS):
        terms = jnp.dot(
            field[i * y_cells : (i + CELLS) * y_cells], right_m[...],
            preferred_element_type=jnp.float32,
        )
        yf_ref[i : i + CELLS] = jnp.sum(
            terms.reshape(CELLS, y_cells, terms.shape[1]) * weights, axis=1
        )
    z_ref[0] = sum(dot_tn(left_x[...], part) for part in three_parts(yf_ref[...]))
    z_ref[1] = sum(
        jnp.dot(part, last_m[...], preferred_element_type=jnp.float32)
        for part in three_parts(cl_ref[...])
    )
    pl.semaphore_wait(barrier, len(greeted))

    z_core = send(z_ref.at[1 - core], z0, other_core)
    y_core = send(yf_ref, y0, other_core)
    for i in range(0, left_x.shape[0], CELLS):
        terms = jnp.dot(
            field[i * y_cells : (i + CELLS) * y_cells], last_m[...],
            preferred_element_type=jnp.float32,
        ).reshape(CELLS, y_cells, 256)
        for c in range(2):
            t_ref[c, i : i + CELLS] = terms[:, :, c * 128 : (c + 1) * 128]
    t_core = {}
    for half in (1, 0):
        for d in (1, 2, 3, 0):
            j0 = pl.multiple_of(((zl + half) % 2) * 32 + ((x + d) % 4) * 8, 8)
            t_core[half, d] = send(
                t_ref.at[1 - core, :, pl.ds(j0, 8)], t0.at[half * 4 + d], other_core
            )
    lx_x = [send(lx_ref, lxall.at[x], at(x_=(x + d) % 4)) for d in range(1, 4)]
    lxall[x] = lx_ref[...]

    z_core.wait_recv()
    zs[...] = z_ref[core] + z0[...]
    z_xy = []
    for d in range(1, 16):
        q, device = peer_xy(d)
        z_xy.append(send(zs.at[pl.ds(pl.multiple_of(q * 8, 8), 8)], z1.at[d], device))
    c_xy = []
    for d in range(1, 16):
        q, device = peer_xy(d)
        c_xy.append(send(cl_ref.at[pl.ds(pl.multiple_of(q * 8, 8), 8)], c1.at[d], device))
    own_xy = pl.ds(pl.multiple_of(pos_xy * 8, 8), 8)

    def t_sum(half, d):
        t_core[half, d].wait_recv()
        j0 = pl.multiple_of(((zl + half) % 2) * 32 + ((x + d) % 4) * 8, 8)
        mine = t_ref[core, :, pl.ds(j0, 8), :]
        ts[half * 4 + d] = (mine + t0[half * 4 + d]).reshape(256, 128)

    t_zl = {}
    for d in (1, 2):
        t_sum(1, d)
        t_zl[d] = send(ts.at[4 + d], t1.at[d], other_zl)
    y_core.wait_recv()
    y0s[...] = yf_ref[...] + y0[...]
    for d in (3, 0):
        t_sum(1, d)
        t_zl[d] = send(ts.at[4 + d], t1.at[d], other_zl)
    for d in (1, 2, 3, 0):
        t_sum(0, d)

    for copy in z_xy:
        copy.wait_recv()
    total = zs[own_xy]
    for d in range(1, 16):
        total = total + z1[d]
    z1s[...] = total
    z_z = []
    for d in range(1, 8):
        z_z.append(send(z1s, z2.at[d], peer_z(d)[1]))
    y_zl = send(y0s, y1, other_zl)

    for copy in c_xy:
        copy.wait_recv()
    total = cl_ref[own_xy]
    for d in range(1, 16):
        total = total + c1[d]
    c1s[...] = total
    t_x = {}

    def t_forward(d):
        t_zl[d].wait_recv()
        t1s[d] = ts[d] + t1[d]
        if d:
            t_x[d] = send(
                t1s.at[d],
                t2.at[pl.ds(pl.multiple_of(x * 256, 256), 256)],
                at(x_=(x + d) % 4),
            )
        else:
            t2[pl.ds(pl.multiple_of(x * 256, 256), 256), :] = t1s[d]

    for d in (1, 2):
        t_forward(d)

    for copy in z_z:
        copy.wait_recv()
    total = z1s[...]
    for d in range(1, 8):
        total = total + z2[d]
    z2s[...] = total
    z_all = []
    for d in range(1, 16):
        z_all.append(send(z2s, zfull.at[own_xy], peer_xy(d)[1]))
    zfull[own_xy] = total
    c_z = [send(c1s, c2.at[d], at(zh_=(zh + d) % 4)) for d in range(1, 4)]
    y_zl.wait_recv()
    y1s[...] = y0s[...] + y1[...]
    y_y = [send(y1s, y2.at[d], at(y_=(y + d) % 4)) for d in range(1, 4)]
    for d in (3, 0):
        t_forward(d)
    for copy in lx_x:
        copy.wait_recv()
    left = dot_nt(
        row_order(128), lxall[...].reshape(128, 128).astype(jnp.bfloat16), None
    ).astype(jnp.bfloat16)

    for copy in z_all:
        copy.wait_recv()
    mat[...] = dot_nt(zfull[...], zfull[...])

    sweep_steps(mat, 0, 32)

    for copy in c_z:
        copy.wait_recv()
    total = c1s[...]
    for d in range(1, 4):
        total = total + c2[d]
    cfull[own_xy] = total
    c_all = []
    for d in range(1, 16):
        c_all.append(send(cfull.at[own_xy], cfull.at[own_xy], peer_xy(d)[1]))
    for copy in t_x.values():
        copy.wait_recv()
    for j in range(8):
        rows = pl.ds(j, 128, stride=8)
        yp[rows, :] = split_dot(left, t2[rows, :])
    t_zh = []
    for d in range(1, 4):
        q = (zh + d) % 4
        t_zh.append(
            send(yp.at[pl.ds(pl.multiple_of(q * 256, 256), 256)], t3.at[d], at(zh_=q))
        )

    sweep_steps(mat, 32, 128)

    inverse = mat[...]
    qall[core] = jnp.dot(
        inverse, zfull[...], precision=HIGHEST, preferred_element_type=jnp.float32
    )
    q_core = send(qall.at[core], qall.at[core], other_core)

    for copy in t_zh:
        copy.wait_recv()
    total = yp[pl.ds(pl.multiple_of(zh * 256, 256), 256), :]
    for d in range(1, 4):
        total = total + t3[d]
    y3[...] = total
    m_core = send(
        y3.at[pl.ds(pl.multiple_of((1 - core) * 128, 128), 128)], y4.at[core], other_core
    )
    y4[core] = y3[pl.ds(pl.multiple_of(core * 128, 128), 128), :]
    for copy in y_y:
        copy.wait_recv()
    total = y1s[...]
    for d in range(1, 4):
        total = total + y2[d]
    q_core.wait_recv()
    m_core.wait_recv()
    mixed = dot_nt(y4[0], qall[1, :, 0:128]) + dot_nt(y4[1], qall[1, :, 128:256])
    mm[...] = mixed.reshape(16, 8, 128)
    m_all = []
    own_j = pl.ds(pl.multiple_of(pos_g * 8, 8), 8)
    for d in range(1, 8):
        q, device = peer_g(d)
        m_all.append(send(mm.at[pl.ds(q * 2, 2)], obuf.at[:, own_j, :], device))
    obuf[:, own_j, :] = mm[pl.ds(pos_g * 2, 2)]
    first_out[...] = dot_nt(total, qall[0])
    for copy in c_all:
        copy.wait_recv()
    last_out[...] = cfull[...]
    for copy in m_all:
        copy.wait_recv()
    middle_out[...] = obuf[...]
    for copy in started:
        copy.wait_send()


COPIES = 1 + 1 + 8 + 3 + 15 + 15 + 4 + 7 + 1 + 3 + 15 + 3 + 3 + 15 + 3 + 1 + 1 + 7


def per_device(flow_field, left_x, last_x, last_y, right_y, right_m, last_m):
    f32 = jnp.float32
    flat_field = flow_field.reshape(-1, flow_field.shape[2])
    inputs = (flat_field, left_x, last_x, last_y, right_y, right_m, last_m)
    shapes = [
        (2, 32, 64, 128), (2, 128, 256), (128, 512), (32, 256), (32, 128),
        (128, 256), (128, 256), (16, 8, 256), (8, 256), (8, 8, 256), (8, 256), (128, 256),
        (2, 128, 256), (128, 128),
        (16, 8, 512), (8, 512), (4, 8, 512), (128, 512),
        (32, 256), (32, 256), (32, 256), (32, 256), (4, 32, 256),
        (4, 32, 128), (8, 32, 8, 128), (8, 256, 128), (4, 256, 128), (4, 256, 128),
        (1024, 128), (1024, 128), (4, 256, 128), (256, 128), (2, 128, 128),
        (16, 8, 128), (2, 64, 128),
    ]
    vmem = pl.BlockSpec(memory_space=pltpu.VMEM)
    return pl.pallas_call(
        exchange_kernel,
        out_shape=(
            jax.ShapeDtypeStruct((32, 128), f32),
            jax.ShapeDtypeStruct((2, 64, 128), f32),
            jax.ShapeDtypeStruct((128, 512), f32),
        ),
        in_specs=[pl.BlockSpec(memory_space=pl.ANY)] * 7,
        out_specs=(vmem,) * 3,
        scratch_shapes=[pltpu.VMEM(array.shape, jnp.bfloat16) for array in inputs]
        + [pltpu.VMEM((2048, 128), jnp.bfloat16)]
        + [pltpu.VMEM(shape, f32) for shape in shapes]
        + [pltpu.SemaphoreType.DMA((count,)) for count in (COPIES, COPIES, 7)],
        compiler_params=pltpu.CompilerParams(
            collective_id=0, has_side_effects=True, vmem_limit_bytes=67_043_328
        ),
        name="exchange",
    )(*inputs)


def solution(mesh):
    return jax.shard_map(
        per_device,
        mesh=mesh,
        in_specs=(
            P("gx", "gy", "gz"),
            P("gx", None),
            P("gx", None),
            P("gy", None),
            P("gy", None),
            P("gz", None),
            P("gz", None),
        ),
        out_specs=(P("gx", None), P(("gx", "gz"), "gy", None), P(None, "gz")),
        check_vma=False,
    )
```
